32 devices in a mesh: px: 16 (over z, x, core), py: 2 (over y).
Axes of the slice: x: 2, y: 2, z: 4, core: 2. Of those that a mesh axis runs over, the one named last changes fastest.
Arguments:
- latents: float32 [32, 4, 128, 512], P('px', 'py'), may hold values from -6 to 6
- cotangent: float32 [32, 4, 128, 512], P('px', 'py'), may hold values from -6 to 6
- w_src: bfloat16 [512, 512], replicated, may hold values from -0.25 to 0.25
- w_dst: bfloat16 [512, 512], replicated, may hold values from -0.25 to 0.25
- b_edge: float32 [512], replicated, may hold values from -3 to 3
- w_msg: bfloat16 [512, 512], replicated, may hold values from -0.25 to 0.25
- w_self: bfloat16 [512, 512], replicated, may hold values from -0.25 to 0.25
- w_agg: bfloat16 [512, 512], replicated, may hold values from -0.25 to 0.25
- b_node: float32 [512], replicated, may hold values from -3 to 3
- w_out: bfloat16 [512, 512], replicated, may hold values from -0.25 to 0.25
- src_block: int32 [16, 2, 12], P('px', 'py'), may hold values from 0 to 11, as said below
- dst_block: int32 [16, 2, 12], P('px', 'py'), may hold values from 0 to 3
- src_node: int32 [16, 2, 12, 128], P('px', 'py'), may hold values from 0 to 127
- dst_node: int32 [16, 2, 12, 128], P('px', 'py'), may hold values from 0 to 127
- long_src: int32 [16, 2, 512], P('px', 'py'), may hold values from 0 to 511, as said below
- long_dst: int32 [16, 2, 512], P('px', 'py'), may hold values from 0 to 511
Outputs:
- grad_latents: float32 [32, 4, 128, 512], P('px', 'py')
- grad_w_src: float32 [512, 512], replicated
- grad_w_dst: float32 [512, 512], replicated
- grad_b_edge: float32 [512], replicated
- grad_w_msg: float32 [512, 512], replicated
- grad_w_self: float32 [512, 512], replicated
- grad_w_agg: float32 [512, 512], replicated
- grad_b_node: float32 [512], replicated
- grad_w_out: float32 [512, 512], replicated
The draws below stay inside these ranges and needn't reach their ends.
Inputs may be any that keep to these rules, and one draw needn't show every extreme that they name: `src_block`: slot numbering as in the reference program: own blocks, then the rim rows before and after, then the rim columns before and after; a patch with py index 0 never names the column before, one with py index 2 - 1 never the column after; for t < 8 (4) tile t names slot 4 + t where that slot is allowed. `long_src`: the coarse edges of one patch come from the coarse nodes of any one patch at most 32 times; in every draw one patch is named exactly 32 times by every patch.
All inputs are finite; a program needn't handle non-finite values.
Results may differ from the reference program's by a relative error of at most 0.011.
Values may be sent and summed in bfloat16 or wider, within the bound.
A program may use at most 128 MiB of HBM per device.

```python
import jax
import jax.numpy as jnp
from jax import lax

D = 512
BLOCK = 128
BX = 2
BY = 2
F_TILES = 12
LONG_E = 512
C_DEV = 16
NBX = 32
NBY = 4
CAP = 32
N_PX = 16
N_PY = 2


def slot_allowed(slot, py_index, inner):
    left_rim = (slot >= inner + 2 * BY) & (slot < inner + 2 * BY + BX)
    right_rim = slot >= inner + 2 * BY + BX
    return jnp.logical_not(left_rim & (py_index == 0) | right_rim & (py_index == N_PY - 1))


def draw_src_block(key, part):
    inner = BX * BY
    rims = 2 * (BX + BY)
    slots = inner + rims
    py_index = jnp.arange(N_PY, dtype=jnp.int32)[None, :, None, None]
    slot = jnp.arange(slots, dtype=jnp.int32)[None, None, None, :]
    allowed = slot_allowed(slot, py_index, inner)
    scores = jax.random.randint(key, (N_PX, N_PY, F_TILES, slots), 0, 65536) * slots + slot
    scores = jnp.where(allowed, scores, -1)
    picked = jnp.argmax(scores, axis=-1).astype(jnp.int32)
    tile = jnp.arange(F_TILES, dtype=jnp.int32)[None, None, :]
    forced = inner + tile
    forced_ok = slot_allowed(forced, py_index[:, :, :, 0], inner) & (tile < rims)
    return jnp.where(forced_ok, forced, picked).astype(jnp.int32)


def draw_long_src(key, part):
    devices = N_PX * N_PY
    slots = devices * CAP
    key_score = jax.random.fold_in(key, 11)
    key_full = jax.random.fold_in(key, 12)
    key_node = jax.random.fold_in(key, 13)
    key_order = jax.random.fold_in(key, 14)
    slot = jnp.arange(slots, dtype=jnp.int32)
    scores = jax.random.randint(key_score, (N_PX, N_PY, slots), 0, 1024) * slots + slot
    full_owner = jax.random.randint(key_full, (), 0, devices)
    scores = jnp.where(slot // CAP == full_owner, scores + 1024 * slots, scores)
    _, chosen = lax_top(scores)
    owner = (chosen // CAP).astype(jnp.int32)
    order_scores = jax.random.randint(key_order, (N_PX, N_PY, LONG_E), 0, 1024) * LONG_E + jnp.arange(LONG_E, dtype=jnp.int32)
    order = jnp.argsort(order_scores, axis=-1, stable=True)
    owner = jnp.take_along_axis(owner, order, axis=-1)
    node = jax.random.randint(key_node, (N_PX, N_PY, LONG_E), 0, C_DEV)
    return (owner * C_DEV + node).astype(jnp.int32)


def lax_top(scores):
    return jax.lax.top_k(scores, LONG_E)


def set_ends(drawn, key, smallest, top_value):
    shape = drawn.shape
    place = [jax.random.randint(jax.random.fold_in(key, axis), (), 0, shape[axis]) for axis in range(len(shape))]
    drawn = drawn.at[tuple(place)].set(smallest)
    longest = shape.index(max(shape))
    place[longest] = (place[longest] + 1) % shape[longest]
    return drawn.at[tuple(place)].set(top_value)


def block_scale(rng, extent, split, smallest, high):
    def one(dim, blocks):
        draws = jax.random.uniform(jax.random.fold_in(jax.random.fold_in(rng, 6), dim), (blocks,), jnp.float32, smallest / len(split), high / len(split))
        return jnp.repeat(jnp.exp(draws), extent[dim] // blocks).reshape((-1,) + (1,) * (len(extent) - dim - 1))

    gain = one(*split[0])
    for cut in split[1:]:
        gain = gain * one(*cut)
    return gain


def centred(rng, shape, deviation, limit, shards=(), kind=jnp.bfloat16):
    array = deviation * jax.random.normal(rng, shape, jnp.float32)
    if shards:
        array = array * block_scale(rng, shape, shards, -0.22, 0.18)
    return jnp.clip(array, -limit, limit).astype(kind)


def setup_inputs(seed: int = 0) -> dict:
    streams_of = jax.random.split(jax.random.key(seed), 17)
    latents = centred(streams_of[0], (NBX, NBY, BLOCK, D), 1.0, 6.0, ((0, 16), (1, 2)), jnp.float32)
    cotangent = centred(streams_of[1], (NBX, NBY, BLOCK, D), 1.0, 6.0, ((0, 16), (1, 2)), jnp.float32)
    w_src = centred(streams_of[2], (D, D), D ** -0.5, 0.25)
    w_dst = centred(streams_of[3], (D, D), D ** -0.5, 0.25)
    b_edge = centred(streams_of[4], (D,), 0.5, 3.0, (), jnp.float32)
    w_msg = centred(streams_of[5], (D, D), D ** -0.5, 0.25)
    w_self = centred(streams_of[6], (D, D), D ** -0.5, 0.25)
    w_agg = centred(streams_of[7], (D, D), D ** -0.5, 0.25)
    b_node = centred(streams_of[8], (D,), 0.5, 3.0, (), jnp.float32)
    w_out = centred(streams_of[9], (D, D), D ** -0.5, 0.25)
    src_block = draw_src_block(jax.random.fold_in(streams_of[16], 71), 0)
    dst_block = set_ends(jax.random.randint(streams_of[11], (N_PX, N_PY, F_TILES), 0, BX * BY), jax.random.fold_in(streams_of[11], 1), 0, (BX * BY) - 1).astype(jnp.int32)
    src_node = set_ends(jax.random.randint(streams_of[12], (N_PX, N_PY, F_TILES, BLOCK), 0, BLOCK), jax.random.fold_in(streams_of[12], 1), 0, BLOCK - 1).astype(jnp.int32)
    dst_node = set_ends(jax.random.randint(streams_of[13], (N_PX, N_PY, F_TILES, BLOCK), 0, BLOCK), jax.random.fold_in(streams_of[13], 1), 0, BLOCK - 1).astype(jnp.int32)
    long_src = draw_long_src(jax.random.fold_in(streams_of[16], 71), 0)
    long_dst = set_ends(jax.random.randint(streams_of[15], (N_PX, N_PY, LONG_E), 0, BX * BY * BLOCK), jax.random.fold_in(streams_of[15], 1), 0, (BX * BY * BLOCK) - 1).astype(jnp.int32)
    return dict(latents=latents, cotangent=cotangent, w_src=w_src, w_dst=w_dst, b_edge=b_edge, w_msg=w_msg, w_self=w_self, w_agg=w_agg, b_node=b_node, w_out=w_out, src_block=src_block, dst_block=dst_block, src_node=src_node, dst_node=dst_node, long_src=long_src, long_dst=long_dst)


def product(left, right):
    return jnp.dot(left, right, preferred_element_type=jnp.float32)


def silu_slope(value):
    sigma = jax.nn.sigmoid(value)
    return sigma * (1.0 + value * (1.0 - sigma))


def as_rounded(value):
    return lax.optimization_barrier(value.astype(jnp.bfloat16)).astype(jnp.float32)


def reference(latents, cotangent, w_src, w_dst, b_edge, w_msg, w_self, w_agg, b_node, w_out, src_block, dst_block, src_node, dst_node, long_src, long_dst):
    rounded = latents.astype(jnp.bfloat16)
    inner = BX * BY
    local_nodes = inner * BLOCK
    stride = local_nodes // C_DEV
    fine_count = F_TILES * BLOCK
    node_ids = jnp.arange(BLOCK, dtype=jnp.int32)
    own = jnp.arange(inner, dtype=jnp.int32)
    across = jnp.arange(BY, dtype=jnp.int32)
    downward = jnp.arange(BX, dtype=jnp.int32)
    zeros_by = jnp.zeros((BY,), jnp.int32)
    zeros_bx = jnp.zeros((BX,), jnp.int32)

    def device_step(carry, device):
        accum, grads = carry
        px_index = device // N_PY
        py_index = device % N_PY
        base_row = px_index * BX
        base_col = py_index * BY
        slot_rows = jnp.concatenate([base_row + own // BY, zeros_by + (base_row - 1) % NBX, zeros_by + (base_row + BX) % NBX, base_row + downward, base_row + downward])
        slot_cols = jnp.concatenate([base_col + own % BY, base_col + across, base_col + across, zeros_bx + jnp.maximum(base_col - 1, 0), zeros_bx + jnp.minimum(base_col + BY, NBY - 1)])
        src_slots = src_block[px_index, py_index]
        dst_slots = dst_block[px_index, py_index]
        src_nodes = src_node[px_index, py_index]
        dst_nodes = dst_node[px_index, py_index]
        src_rows = slot_rows[src_slots][:, None]
        src_cols = slot_cols[src_slots][:, None]
        fine_src = rounded[src_rows, src_cols, src_nodes]
        dst_rows = (base_row + dst_slots // BY)[:, None]
        dst_cols = (base_col + dst_slots % BY)[:, None]
        fine_dst = rounded[dst_rows, dst_cols, dst_nodes]
        long_from = long_src[px_index, py_index]
        owner = long_from // C_DEV
        offset = (long_from % C_DEV) * stride
        owner_block = offset // BLOCK
        long_rows = (owner // N_PY) * BX + owner_block // BY
        long_cols = (owner % N_PY) * BY + owner_block % BY
        long_node = offset % BLOCK
        long_sender = rounded[long_rows, long_cols, long_node]
        long_into = long_dst[px_index, py_index]
        into_block = long_into // BLOCK
        into_rows = base_row + into_block // BY
        into_cols = base_col + into_block % BY
        into_node = long_into % BLOCK
        long_receiver = rounded[into_rows, into_cols, into_node]
        sender = jnp.concatenate([fine_src.reshape(fine_count, D), long_sender], axis=0)
        receiver = jnp.concatenate([fine_dst.reshape(fine_count, D), long_receiver], axis=0)
        pre_edge = product(sender, w_src) + product(receiver, w_dst) + b_edge
        edge_act = jax.nn.silu(pre_edge).astype(jnp.bfloat16)
        message = product(edge_act, w_msg).astype(jnp.bfloat16)
        dst_flat = jnp.concatenate([(dst_slots[:, None] * BLOCK + dst_nodes).reshape(fine_count), long_into])
        incoming = jnp.zeros((local_nodes, D), jnp.float32).at[dst_flat].add(message.astype(jnp.float32))
        incoming_b = incoming.astype(jnp.bfloat16)
        start = (base_row, base_col, jnp.int32(0), jnp.int32(0))
        own_rows = lax.dynamic_slice(rounded, start, (BX, BY, BLOCK, D)).reshape(local_nodes, D)
        node_pre = product(own_rows, w_self) + product(incoming_b, w_agg) + b_node
        node_act = jax.nn.silu(node_pre).astype(jnp.bfloat16)
        cot_local = lax.dynamic_slice(cotangent, start, (BX, BY, BLOCK, D)).reshape(local_nodes, D).astype(jnp.bfloat16)
        d_out = product(node_act.T, cot_local)
        g_node = (product(cot_local, w_out.T) * silu_slope(node_pre)).astype(jnp.bfloat16)
        d_self = product(own_rows.T, g_node)
        d_agg = product(incoming_b.T, g_node)
        d_bnode = jnp.sum(g_node.astype(jnp.float32), axis=0)
        g_self = product(g_node, w_self.T)
        g_incoming = product(g_node, w_agg.T).astype(jnp.bfloat16)
        g_message = g_incoming[dst_flat]
        d_msg = product(edge_act.T, g_message)
        g_pre = (product(g_message, w_msg.T) * silu_slope(pre_edge)).astype(jnp.bfloat16)
        d_src = product(sender.T, g_pre)
        d_dst = product(receiver.T, g_pre)
        d_bedge = jnp.sum(g_pre.astype(jnp.float32), axis=0)
        g_send = as_rounded(product(g_pre, w_src.T))
        g_recv = as_rounded(product(g_pre, w_dst.T))
        accum = accum.at[src_rows, src_cols, src_nodes].add(g_send[:fine_count].reshape(F_TILES, BLOCK, D))
        accum = accum.at[long_rows, long_cols, long_node].add(g_send[fine_count:])
        accum = accum.at[dst_rows, dst_cols, dst_nodes].add(g_recv[:fine_count].reshape(F_TILES, BLOCK, D))
        accum = accum.at[into_rows, into_cols, into_node].add(g_recv[fine_count:])
        self_rows = (base_row + own // BY)[:, None]
        self_cols = (base_col + own % BY)[:, None]
        accum = accum.at[self_rows, self_cols, node_ids[None, :]].add(g_self.reshape(inner, BLOCK, D))
        terms = (d_src, d_dst, d_bedge, d_msg, d_self, d_agg, d_bnode, d_out)
        grads = tuple(total + term for total, term in zip(grads, terms))
        return (accum, grads), None

    matrix_zero = jnp.zeros((D, D), jnp.float32)
    vector_zero = jnp.zeros((D,), jnp.float32)
    grads = (matrix_zero, matrix_zero, vector_zero, matrix_zero, matrix_zero, matrix_zero, vector_zero, matrix_zero)
    accum = jnp.zeros((NBX, NBY, BLOCK, D), jnp.float32)
    devices = jnp.arange(N_PX * N_PY, dtype=jnp.int32)
    (accum, grads), _ = lax.scan(device_step, (accum, grads), devices)
    grad_latents = cotangent + accum
    return (grad_latents, grads[0], grads[1], grads[2], grads[3], grads[4], grads[5], grads[6], grads[7])
```

```python
import functools

import jax
import jax.numpy as jnp
from jax import lax
from jax.experimental import pallas as pl
from jax.experimental.pallas import tpu as pltpu
from jax.sharding import PartitionSpec as P

C_DEV = 16
GROUP = 4
LANES = 128
MESH = pl.DeviceIdType.MESH
F32 = jnp.float32
BF16 = jnp.bfloat16


def bits_of(size):
    return size.bit_length() - 1


def step_list(n_px, n_py, px, py):
    core = px % 2
    px_bits = list(range(1, bits_of(n_px)))
    py_bits = list(range(bits_of(n_py)))

    def px_step(bit):
        mine = (px // (1 << bit)) % 2
        return mine, (1 - 2 * mine) * (1 << bit)

    def py_step(bit):
        mine = (py // (1 << bit)) % 2
        return mine, (1 - 2 * mine) * (1 << bit)

    steps = []
    mine, move = px_step(0)
    steps.append((mine, px + move, py))
    while px_bits and py_bits:
        mine_x, move_x = px_step(px_bits.pop(0))
        mine_y, move_y = py_step(py_bits.pop(0))
        for pick in (core, 1 - core):
            other = 1 - pick
            steps.append(
                (other * mine_x + pick * mine_y, px + other * move_x, py + pick * move_y)
            )
    for bit in px_bits:
        mine, move = px_step(bit)
        steps.append((mine, px + move, py))
    for bit in py_bits:
        mine, move = py_step(bit)
        steps.append((mine, px, py + move))
    return steps


def position_of(n_px, n_py, px, py):
    place = 0
    for mine, _, _ in step_list(n_px, n_py, px, py):
        place = place * 2 + mine
    return place


def greet(partners, edges, beside):
    barrier = pltpu.get_barrier_semaphore()
    for device in partners:
        pl.semaphore_signal(barrier, inc=1, device_id=device, device_id_type=MESH)
    for condition, device in edges:

        @pl.when(condition)
        def _(device=device):
            pl.semaphore_signal(barrier, inc=1, device_id=device, device_id_type=MESH)

    pl.semaphore_wait(barrier, len(partners) + beside)


def spread_kernel(n_px, n_py, own, coarse, rim, table, send, recv, rim_send, rim_recv):
    px, py = lax.axis_index("px"), lax.axis_index("py")
    rows_x, rows_y = own.shape[:2]
    steps = step_list(n_px, n_py, px, py)
    above, below = (lax.rem(px + n_px - 1, n_px), py), (lax.rem(px + 1, n_px), py)
    before, after = (px, py - 1), (px, py + 1)
    has_before, has_after = py > 0, py < n_py - 1
    beside = (py + n_py - 1) // n_py + (2 * n_py - 2 - py) // n_py
    greet(
        [(a, b) for _, a, b in steps] + [above, below],
        [(has_before, before), (has_after, after)],
        beside,
    )

    def rim_copy(which, source, start, count, device):
        return pltpu.make_async_remote_copy(
            src_ref=source,
            dst_ref=rim.at[pl.ds(start, count)],
            send_sem=rim_send.at[which],
            recv_sem=rim_recv.at[which],
            device_id=device,
            device_id_type=MESH,
        )

    down = rim_copy(0, own.at[rows_x - 1], 0, rows_y, below)
    up = rim_copy(1, own.at[0], rows_y, rows_y, above)
    right = rim_copy(2, own.at[:, rows_y - 1], 2 * rows_y, rows_x, after)
    left = rim_copy(3, own.at[:, 0], 2 * rows_y + rows_x, rows_x, before)
    chunk = coarse.shape[0]
    base = position_of(n_px, n_py, px, py)
    table[pl.ds(pl.multiple_of(base * chunk, chunk), chunk), :] = coarse[...]
    for k, (mine, a, b) in enumerate(reversed(steps)):
        if k == 0:
            source = coarse
        else:
            source = table.at[pl.ds(pl.multiple_of(base * chunk, chunk), chunk << k)]
        copy = pltpu.make_async_remote_copy(
            src_ref=source,
            dst_ref=table.at[pl.ds(pl.multiple_of(base * chunk, chunk), chunk << k)],
            send_sem=send.at[k],
            recv_sem=recv.at[k],
            device_id=(a, b),
            device_id_type=MESH,
        )
        copy.start()
        if k == 0:
            down.start()
            up.start()
            pl.when(has_after)(right.start)
            pl.when(has_before)(left.start)

            @pl.when(jnp.logical_not(has_before))
            def _():
                rim[2 * rows_y : 2 * rows_y + rows_x] = jnp.zeros((rows_x,) + rim.shape[1:], BF16)

            @pl.when(jnp.logical_not(has_after))
            def _():
                rim[2 * rows_y + rows_x :] = jnp.zeros((rows_x,) + rim.shape[1:], BF16)

        copy.wait()
        base = base - mine * (1 << k)
    down.wait()
    up.wait()
    pl.when(has_after)(right.wait_send)
    pl.when(has_before)(right.wait_recv)
    pl.when(has_before)(left.wait_send)
    pl.when(has_after)(left.wait_recv)


def reduce_kernel(
    n_px, n_py, rows_x, rows_y, w_in, c_in, rim, w_out, c_out, rec,
    w_acc, w_got, c_acc, c_got, sems, c_sems, rim_sems, g_sems,
):
    px, py = lax.axis_index("px"), lax.axis_index("py")
    steps = step_list(n_px, n_py, px, py)
    count = len(steps)
    above, below = (lax.rem(px + n_px - 1, n_px), py), (lax.rem(px + 1, n_px), py)
    before, after = (px, py - 1), (px, py + 1)
    has_before, has_after = py > 0, py < n_py - 1
    beside = (py + n_py - 1) // n_py + (2 * n_py - 2 - py) // n_py
    greet(
        [(a, b) for _, a, b in steps] + [above, below],
        [(has_before, before), (has_after, after)],
        beside,
    )

    def rim_copy(which, start, size, device):
        return pltpu.make_async_remote_copy(
            src_ref=rim.at[pl.ds(start, size)],
            dst_ref=rec.at[pl.ds(start, size)],
            send_sem=rim_sems.at[0, which],
            recv_sem=rim_sems.at[1, which],
            device_id=device,
            device_id_type=MESH,
        )

    up = rim_copy(0, 0, rows_y, above)
    down = rim_copy(1, rows_y, rows_y, below)
    left = rim_copy(2, 2 * rows_y, rows_x, before)
    right = rim_copy(3, 2 * rows_y + rows_x, rows_x, after)

    def add_into(target, start, source, source_start, extra, extra_start, rows, piece):
        @pl.loop(0, rows // piece)
        def _(i):
            shift = i * piece
            first = source[pl.ds(pl.multiple_of(source_start + shift, 16), piece), :].astype(F32)
            second = extra[pl.ds(pl.multiple_of(extra_start + shift, 16), piece), :].astype(F32)
            target[pl.ds(pl.multiple_of(start + shift, 16), piece), :] = (first + second).astype(BF16)

    w_last = w_in.shape[0] >> count
    c_last = c_in.shape[0] >> count
    w_off, c_off = 0, 0
    got = 0
    c_at = 0
    offsets = []
    for s, (mine, a, b) in enumerate(steps):
        w_half = w_in.shape[0] >> (s + 1)
        c_half = c_in.shape[0] >> (s + 1)
        w_from, c_from = (w_in, c_in) if s == 0 else (w_acc, c_acc)
        w_keep, w_send = w_off + mine * w_half, w_off + (1 - mine) * w_half
        c_keep, c_send = c_off + mine * c_half, c_off + (1 - mine) * c_half
        w_copy = pltpu.make_async_remote_copy(
            src_ref=w_from.at[pl.ds(pl.multiple_of(w_send, 16), w_half)],
            dst_ref=w_got.at[pl.ds(got, w_half)],
            send_sem=sems.at[0, s],
            recv_sem=sems.at[1, s],
            device_id=(a, b),
            device_id_type=MESH,
        )
        c_copy = pltpu.make_async_remote_copy(
            src_ref=c_from.at[pl.ds(pl.multiple_of(c_send, 16), c_half)],
            dst_ref=c_got.at[pl.ds(c_at, c_half)],
            send_sem=c_sems.at[0, s],
            recv_sem=c_sems.at[1, s],
            device_id=(a, b),
            device_id_type=MESH,
        )
        c_copy.start()
        w_copy.start()
        if s == 1:
            up.start()
            down.start()
            pl.when(has_before)(left.start)
            pl.when(has_after)(right.start)

            @pl.when(jnp.logical_not(has_after))
            def _():
                rec[2 * rows_y : 2 * rows_y + rows_x] = jnp.zeros((rows_x,) + rec.shape[1:], BF16)

            @pl.when(jnp.logical_not(has_before))
            def _():
                rec[2 * rows_y + rows_x :] = jnp.zeros((rows_x,) + rec.shape[1:], BF16)

        final = s == count - 1
        c_copy.wait()
        if final:
            c_out[...] = (
                c_acc[pl.ds(pl.multiple_of(c_keep, 16), c_last), :].astype(F32)
                + c_got[pl.ds(c_at, c_last), :].astype(F32)
            ).astype(BF16)
        else:
            add_into(c_acc, c_keep, c_from, c_keep, c_got, c_at, c_half, c_last)
        w_copy.wait()
        add_into(w_out if final else w_acc, w_keep, w_from, w_keep, w_got, got, w_half, w_last)
        got += w_half
        c_at += c_half
        w_off, c_off = w_keep, c_keep
        offsets.append(w_keep)
    for k, (mine, a, b) in enumerate(reversed(steps)):
        s = count - 1 - k
        region = w_out.at[pl.ds(pl.multiple_of(offsets[s], 16), w_in.shape[0] >> (s + 1))]
        copy = pltpu.make_async_remote_copy(
            src_ref=region,
            dst_ref=region,
            send_sem=g_sems.at[0, k],
            recv_sem=g_sems.at[1, k],
            device_id=(a, b),
            device_id_type=MESH,
        )
        copy.start()
        copy.wait()
    up.wait()
    down.wait()
    pl.when(has_before)(left.wait_send)
    pl.when(has_after)(left.wait_recv)
    pl.when(has_after)(right.wait_send)
    pl.when(has_before)(right.wait_recv)


def dot(left, right):
    return jnp.dot(left, right, preferred_element_type=F32)


def dot_t(left, right):
    return lax.dot_general(left, right, (((0,), (0,)), ((), ())), preferred_element_type=F32)


def dot_nt(left, right):
    return lax.dot_general(left, right, (((1,), (1,)), ((), ())), preferred_element_type=F32)


def silu_and_slope(value):
    sigma = jax.nn.sigmoid(value)
    return value * sigma, sigma * (1.0 + value * (1.0 - sigma))


def local_kernel(
    src_block, dst_block, own, rim, coarse, cot, w_src, w_dst, b_edge, w_msg, w_self, w_agg,
    b_node, w_out, src_idx, dst_idx, long_src, long_dst,
    base, g_own, g_rim, g_coarse, weights,
    table, sender, pre, act_sum, g_dst, g_table, half, d_src, d_bias,
):
    inner, block, width = own.shape
    rows = inner * block
    tiles = src_idx.shape[0]
    long_count = long_src.shape[1]
    span = GROUP * block
    table[:inner] = own[...]
    table[inner:] = rim[...]
    g_table[...] = jnp.zeros_like(g_table)
    g_dst[...] = jnp.zeros_like(g_dst)
    act_sum[...] = jnp.zeros_like(act_sum)
    d_src[...] = jnp.zeros_like(d_src)
    d_bias[...] = jnp.zeros_like(d_bias)
    own_rows = own[...].reshape(rows, width)
    half[...] = dot(own_rows, w_dst[...]).astype(BF16).reshape(inner, block, width)

    def hot(index, nodes):
        count = index.shape[1]
        return (lax.broadcasted_iota(jnp.int32, (nodes, count), 0) == index).astype(BF16)

    @pl.loop(0, tiles // GROUP)
    def _(g):
        first = pl.multiple_of(g * span, span)
        for j in range(GROUP):
            t = g * GROUP + j
            at = pl.ds(pl.multiple_of(first + j * block, block), block)
            sender[at, :] = dot_t(hot(src_idx[t], block), table[src_block[t]]).astype(BF16)
            pre[at, :] = dot_t(hot(dst_idx[t], block), half[dst_block[t]])
        at = pl.ds(first, span)
        value = dot(sender[at, :], w_src[...]) + pre[at, :] + b_edge[...]
        pre[at, :] = value
        act = (value * jax.nn.sigmoid(value)).astype(BF16)
        for j in range(GROUP):
            t = g * GROUP + j
            act_sum[dst_block[t]] += dot(
                hot(dst_idx[t], block), act[j * block : (j + 1) * block]
            )

    fine = tiles * block
    long_at = slice(fine, fine + long_count)
    long_hot = hot(long_dst[...], rows)
    sender[long_at, :] = dot_t(hot(long_src[...], coarse.shape[0]), coarse[...]).astype(BF16)
    value = (
        dot(sender[long_at, :], w_src[...])
        + dot_t(long_hot, half[...].reshape(rows, width))
        + b_edge[...]
    )
    pre[long_at, :] = value
    act = (value * jax.nn.sigmoid(value)).astype(BF16)
    acts = (act_sum[...].reshape(rows, width) + dot(long_hot, act)).astype(BF16)
    incoming = dot(acts, w_msg[...]).astype(BF16)
    node_pre = dot(own_rows, w_self[...]) + dot(incoming, w_agg[...]) + b_node[...]
    node_silu, node_slope = silu_and_slope(node_pre)
    cot_rows = cot[...].reshape(rows, width)
    cot_b = cot_rows.astype(BF16)

    def put(which, value):
        value = value.astype(BF16)
        for j in range(width // LANES):
            start = (which * (width // LANES) + j) * width
            weights[start : start + width, :] = value[:, j * LANES : (j + 1) * LANES]

    put(5, dot_t(node_silu.astype(BF16), cot_b))
    g_node = (dot_nt(cot_b, w_out[...]) * node_slope).astype(BF16)
    put(3, dot_t(own_rows, g_node))
    put(4, dot_t(incoming, g_node))
    d_node = jnp.sum(g_node.astype(F32), axis=0, keepdims=True)
    g_incoming = dot_nt(g_node, w_agg[...]).astype(BF16)
    put(2, dot_t(acts, g_incoming))
    base[...] = (cot_rows + dot_nt(g_node, w_self[...])).reshape(inner, block, width)
    half[...] = dot_nt(g_incoming, w_msg[...]).astype(BF16).reshape(inner, block, width)

    @pl.loop(0, tiles // GROUP)
    def _(g):
        first = pl.multiple_of(g * span, span)
        for j in range(GROUP):
            t = g * GROUP + j
            at = pl.ds(pl.multiple_of(first + j * block, block), block)
            dst_hot = hot(dst_idx[t], block)
            _, slope = silu_and_slope(pre[at, :])
            g_pre = (dot_t(dst_hot, half[dst_block[t]]) * slope).astype(BF16)
            pre[at, :] = g_pre.astype(F32)
            g_dst[dst_block[t]] += dot(dst_hot, g_pre)
            g_table[src_block[t]] += dot(hot(src_idx[t], block), g_pre)
        at = pl.ds(first, span)
        whole = pre[at, :]
        d_src[...] += dot_t(sender[at, :], whole.astype(BF16))
        d_bias[...] += jnp.sum(whole, axis=0, keepdims=True)

    _, slope = silu_and_slope(pre[long_at, :])
    long_hot = hot(long_dst[...], rows)
    g_pre = (dot_t(long_hot, half[...].reshape(rows, width)) * slope).astype(BF16)
    g_coarse[...] = dot(hot(long_src[...], coarse.shape[0]), g_pre).astype(BF16)
    put(0, d_src[...] + dot_t(sender[long_at, :], g_pre))
    d_edge = d_bias[...] + jnp.sum(g_pre.astype(F32), axis=0, keepdims=True)
    g_recv = (g_dst[...].reshape(rows, width) + dot(long_hot, g_pre)).astype(BF16)
    put(1, dot_t(own_rows, g_recv))
    base[...] += dot_nt(g_recv, w_dst[...]).reshape(inner, block, width)
    g_own[...] = g_table[:inner]
    g_rim[...] = g_table[inner:].astype(BF16)
    start = 6 * width * (width // LANES)
    tail = weights.shape[0] - start
    weights[start:, :] = jnp.zeros((tail, LANES), BF16)
    parts = [v[:, j * LANES : (j + 1) * LANES] for v in (d_edge, d_node) for j in range(width // LANES)]
    parts.append(jnp.zeros((16 - len(parts), LANES), F32))
    weights[start : start + 16, :] = jnp.concatenate(parts, axis=0).astype(BF16)


def finish_kernel(
    rows_x, rows_y, base, g_own, rec, c_sum, w_src, weights,
    grad, d_src, d_dst, b_edge, d_msg, d_self, d_agg, b_node, d_out, total,
):
    inner, block, width = base.shape
    rows = inner * block
    count = c_sum.shape[0]
    stride = rows // count
    node = lax.broadcasted_iota(jnp.int32, (rows, count), 0)
    place = lax.broadcasted_iota(jnp.int32, (rows, count), 1) * stride
    pick = (node == place).astype(BF16)
    total[...] = g_own[...] + dot(pick, c_sum[...]).reshape(inner, block, width)
    for c in range(rows_y):
        total[(rows_x - 1) * rows_y + c] += rec[c].astype(F32)
        total[c] += rec[rows_y + c].astype(F32)
    for r in range(rows_x):
        total[r * rows_y + rows_y - 1] += rec[2 * rows_y + r].astype(F32)
        total[r * rows_y] += rec[2 * rows_y + rows_x + r].astype(F32)
    sent = total[...].reshape(rows, width).astype(BF16)
    grad[...] = base[...] + dot_nt(sent, w_src[...]).reshape(inner, block, width)
    cols = width // LANES
    for which, ref in enumerate((d_src, d_dst, d_msg, d_self, d_agg, d_out)):
        for j in range(cols):
            start = (which * cols + j) * width
            ref[:, j * LANES : (j + 1) * LANES] = weights[start : start + width, :].astype(F32)
    start = 6 * width * cols
    bias = weights[start : start + 16, :].astype(F32)
    for j in range(cols):
        b_edge[:, j * LANES : (j + 1) * LANES] = bias[j : j + 1]
        b_node[:, j * LANES : (j + 1) * LANES] = bias[cols + j : cols + j + 1]


def vmem(count):
    return [pl.BlockSpec(memory_space=pltpu.VMEM)] * count


def body(
    n_px, n_py, latents, cotangent, w_src, w_dst, b_edge, w_msg, w_self, w_agg, b_node, w_out,
    src_block, dst_block, src_node, dst_node, long_src, long_dst,
):
    rows_x, rows_y, block, width = latents.shape
    inner = rows_x * rows_y
    nodes = inner * block
    rims = 2 * (rows_x + rows_y)
    tiles = src_block.shape[-1]
    long_count = long_src.shape[-1]
    edges = tiles * block + long_count
    devices = n_px * n_py
    stride = nodes // C_DEV
    steps = bits_of(n_px) + bits_of(n_py)
    coarse_count = C_DEV * devices
    exact = 6 * width * width // LANES + 16
    unit = 16 * devices
    w_rows = -(-exact // unit) * unit
    shape = jax.ShapeDtypeStruct
    dma = pltpu.SemaphoreType.DMA

    rounded = latents.astype(BF16)
    coarse_rows = latents.reshape(nodes, width)[::stride].astype(BF16)
    rim, coarse = pl.pallas_call(
        functools.partial(spread_kernel, n_px, n_py),
        out_shape=(shape((rims, block, width), BF16), shape((coarse_count, width), BF16)),
        in_specs=vmem(2),
        out_specs=tuple(vmem(2)),
        scratch_shapes=[dma((steps,)), dma((steps,)), dma((4,)), dma((4,))],
        compiler_params=pltpu.CompilerParams(collective_id=0, has_side_effects=True),
        name="spread",
    )(rounded, coarse_rows)

    owner = long_src.reshape(1, long_count) // C_DEV
    place = position_of(n_px, n_py, owner // n_py, owner % n_py)
    long_place = place * C_DEV + long_src.reshape(1, long_count) % C_DEV

    smem = [pl.BlockSpec(memory_space=pltpu.SMEM)] * 2
    base, g_own, g_rim, g_coarse, weights = pl.pallas_call(
        local_kernel,
        out_shape=(
            shape((inner, block, width), F32),
            shape((inner, block, width), F32),
            shape((rims, block, width), BF16),
            shape((coarse_count, width), BF16),
            shape((w_rows, LANES), BF16),
        ),
        in_specs=smem + vmem(16),
        out_specs=tuple(vmem(5)),
        scratch_shapes=[
            pltpu.VMEM((inner + rims, block, width), BF16),
            pltpu.VMEM((edges, width), BF16),
            pltpu.VMEM((edges, width), F32),
            pltpu.VMEM((inner, block, width), F32),
            pltpu.VMEM((inner, block, width), F32),
            pltpu.VMEM((inner + rims, block, width), F32),
            pltpu.VMEM((inner, block, width), BF16),
            pltpu.VMEM((width, width), F32),
            pltpu.VMEM((1, width), F32),
        ],
        compiler_params=pltpu.CompilerParams(vmem_limit_bytes=60 * 1024 * 1024),
        name="local",
    )(
        src_block.reshape(tiles), dst_block.reshape(tiles),
        rounded.reshape(inner, block, width), rim, coarse,
        cotangent.reshape(inner, block, width),
        w_src, w_dst, b_edge.reshape(1, width), w_msg, w_self, w_agg, b_node.reshape(1, width),
        w_out, src_node.reshape(tiles, 1, block), dst_node.reshape(tiles, 1, block),
        long_place, long_dst.reshape(1, long_count),
    )

    w_sum, c_sum, rec = pl.pallas_call(
        functools.partial(reduce_kernel, n_px, n_py, rows_x, rows_y),
        out_shape=(
            shape((w_rows, LANES), BF16),
            shape((C_DEV, width), BF16),
            shape((rims, block, width), BF16),
        ),
        in_specs=vmem(3),
        out_specs=tuple(vmem(3)),
        scratch_shapes=[
            pltpu.VMEM((w_rows, LANES), BF16),
            pltpu.VMEM((w_rows, LANES), BF16),
            pltpu.VMEM((coarse_count, width), BF16),
            pltpu.VMEM((coarse_count, width), BF16),
            dma((2, steps)), dma((2, steps)), dma((2, 4)), dma((2, steps)),
        ],
        compiler_params=pltpu.CompilerParams(
            collective_id=1, has_side_effects=True, vmem_limit_bytes=60 * 1024 * 1024
        ),
        name="reduce",
    )(weights, g_coarse, g_rim)

    matrix, vector = shape((width, width), F32), shape((1, width), F32)
    grad, d_src, d_dst, d_edge, d_msg, d_self, d_agg, d_node, d_out = pl.pallas_call(
        functools.partial(finish_kernel, rows_x, rows_y),
        out_shape=(
            shape((inner, block, width), F32),
            matrix, matrix, vector, matrix, matrix, matrix, vector, matrix,
        ),
        in_specs=vmem(6),
        out_specs=tuple(vmem(9)),
        scratch_shapes=[pltpu.VMEM((inner, block, width), F32)],
        compiler_params=pltpu.CompilerParams(vmem_limit_bytes=60 * 1024 * 1024),
        name="finish",
    )(base, g_own, rec, c_sum, w_src, w_sum)
    return (
        grad.reshape(latents.shape), d_src, d_dst, d_edge.reshape(width), d_msg, d_self, d_agg,
        d_node.reshape(width), d_out,
    )


def solution(mesh):
    n_px, n_py = mesh.shape["px"], mesh.shape["py"]
    part = {4: P("px", "py", None, None), 3: P("px", "py", None)}
    in_specs = (part[4], part[4]) + (P(),) * 8 + (part[3], part[3], part[4], part[4], part[3], part[3])
    out_specs = (part[4],) + (P(),) * 8
    return jax.shard_map(
        functools.partial(body, n_px, n_py),
        mesh=mesh, in_specs=in_specs, out_specs=out_specs, check_vma=False,
    )
```

```python
import functools

import jax
import jax.numpy as jnp
from jax import lax
from jax.experimental import pallas as pl
from jax.experimental.pallas import tpu as pltpu
from jax.sharding import PartitionSpec as P

C_DEV = 16
GROUP = 4
CHUNKS = 4
COARSE_DELAY = 2
LANES = 128
MESH = pl.DeviceIdType.MESH
F32 = jnp.float32
BF16 = jnp.bfloat16


def bits_of(size):
    return size.bit_length() - 1


def step_list(n_px, n_py, px, py):
    core = px % 2
    px_bits = list(range(1, bits_of(n_px)))
    py_bits = list(range(bits_of(n_py)))

    def px_step(bit):
        mine = (px // (1 << bit)) % 2
        return mine, (1 - 2 * mine) * (1 << bit)

    def py_step(bit):
        mine = (py // (1 << bit)) % 2
        return mine, (1 - 2 * mine) * (1 << bit)

    steps = []
    mine, move = px_step(0)
    steps.append((mine, px + move, py))
    while px_bits and py_bits:
        mine_x, move_x = px_step(px_bits.pop(0))
        mine_y, move_y = py_step(py_bits.pop(0))
        for pick in (core, 1 - core):
            other = 1 - pick
            steps.append(
                (other * mine_x + pick * mine_y, px + other * move_x, py + pick * move_y)
            )
    for bit in px_bits:
        mine, move = px_step(bit)
        steps.append((mine, px + move, py))
    for bit in py_bits:
        mine, move = py_step(bit)
        steps.append((mine, px, py + move))
    return steps


def position_of(n_px, n_py, px, py):
    place = 0
    for mine, _, _ in step_list(n_px, n_py, px, py):
        place = place * 2 + mine
    return place


def greet(partners, edges, beside):
    barrier = pltpu.get_barrier_semaphore()
    for device in partners:
        pl.semaphore_signal(barrier, inc=1, device_id=device, device_id_type=MESH)
    for condition, device in edges:

        @pl.when(condition)
        def _(device=device):
            pl.semaphore_signal(barrier, inc=1, device_id=device, device_id_type=MESH)

    pl.semaphore_wait(barrier, len(partners) + beside)


def spread_kernel(n_px, n_py, own, coarse, rim, table, send, recv, rim_send, rim_recv):
    px, py = lax.axis_index("px"), lax.axis_index("py")
    rows_x, rows_y = own.shape[:2]
    steps = step_list(n_px, n_py, px, py)
    above, below = (lax.rem(px + n_px - 1, n_px), py), (lax.rem(px + 1, n_px), py)
    before, after = (px, py - 1), (px, py + 1)
    has_before, has_after = py > 0, py < n_py - 1
    beside = (py + n_py - 1) // n_py + (2 * n_py - 2 - py) // n_py
    greet(
        [(a, b) for _, a, b in steps] + [above, below],
        [(has_before, before), (has_after, after)],
        beside,
    )

    def rim_copy(which, source, start, count, device):
        return pltpu.make_async_remote_copy(
            src_ref=source,
            dst_ref=rim.at[pl.ds(start, count)],
            send_sem=rim_send.at[which],
            recv_sem=rim_recv.at[which],
            device_id=device,
            device_id_type=MESH,
        )

    down = rim_copy(0, own.at[rows_x - 1], 0, rows_y, below)
    up = rim_copy(1, own.at[0], rows_y, rows_y, above)
    right = rim_copy(2, own.at[:, rows_y - 1], 2 * rows_y, rows_x, after)
    left = rim_copy(3, own.at[:, 0], 2 * rows_y + rows_x, rows_x, before)
    chunk = coarse.shape[0]
    base = position_of(n_px, n_py, px, py)
    table[pl.ds(pl.multiple_of(base * chunk, chunk), chunk), :] = coarse[...]
    for k, (mine, a, b) in enumerate(reversed(steps)):
        if k == 0:
            source = coarse
        else:
            source = table.at[pl.ds(pl.multiple_of(base * chunk, chunk), chunk << k)]
        copy = pltpu.make_async_remote_copy(
            src_ref=source,
            dst_ref=table.at[pl.ds(pl.multiple_of(base * chunk, chunk), chunk << k)],
            send_sem=send.at[k],
            recv_sem=recv.at[k],
            device_id=(a, b),
            device_id_type=MESH,
        )
        copy.start()
        if k == 0:
            down.start()
            up.start()
            pl.when(has_after)(right.start)
            pl.when(has_before)(left.start)

            @pl.when(jnp.logical_not(has_before))
            def _():
                rim[2 * rows_y : 2 * rows_y + rows_x] = jnp.zeros((rows_x,) + rim.shape[1:], BF16)

            @pl.when(jnp.logical_not(has_after))
            def _():
                rim[2 * rows_y + rows_x :] = jnp.zeros((rows_x,) + rim.shape[1:], BF16)

        copy.wait()
        base = base - mine * (1 << k)
    down.wait()
    up.wait()
    pl.when(has_after)(right.wait_send)
    pl.when(has_before)(right.wait_recv)
    pl.when(has_before)(left.wait_send)
    pl.when(has_after)(left.wait_recv)


def reduce_kernel(
    n_px, n_py, rows_x, rows_y, w_in, c_in, rim, w_out, c_out, rec,
    w_acc, w_got, c_acc, c_got, sems, rim_sems,
):
    px, py = lax.axis_index("px"), lax.axis_index("py")
    steps = step_list(n_px, n_py, px, py)
    count = len(steps)
    above, below = (lax.rem(px + n_px - 1, n_px), py), (lax.rem(px + 1, n_px), py)
    before, after = (px, py - 1), (px, py + 1)
    has_before, has_after = py > 0, py < n_py - 1
    beside = (py + n_py - 1) // n_py + (2 * n_py - 2 - py) // n_py
    greet(
        [(a, b) for _, a, b in steps] + [above, below],
        [(has_before, before), (has_after, after)],
        beside,
    )

    def rim_copy(which, start, size, device):
        return pltpu.make_async_remote_copy(
            src_ref=rim.at[pl.ds(start, size)],
            dst_ref=rec.at[pl.ds(start, size)],
            send_sem=rim_sems.at[0, which],
            recv_sem=rim_sems.at[1, which],
            device_id=device,
            device_id_type=MESH,
        )

    up = rim_copy(0, 0, rows_y, above)
    down = rim_copy(1, rows_y, rows_y, below)
    left = rim_copy(2, 2 * rows_y, rows_x, before)
    right = rim_copy(3, 2 * rows_y + rows_x, rows_x, after)

    def add_into(target, start, source, source_start, extra, extra_start, rows, piece):
        @pl.loop(0, rows // piece)
        def _(i):
            shift = i * piece
            first = source[pl.ds(pl.multiple_of(source_start + shift, 16), piece), :].astype(F32)
            second = extra[pl.ds(pl.multiple_of(extra_start + shift, 16), piece), :].astype(F32)
            target[pl.ds(pl.multiple_of(start + shift, 16), piece), :] = (first + second).astype(BF16)

    unit = 16 << count
    units = w_in.shape[0] // unit
    streams = []
    start = 0
    for c in range(CHUNKS):
        rows = (units // CHUNKS + (1 if c < units % CHUNKS else 0)) * unit
        if rows:
            streams.append(
                dict(delay=c, first=start, rows=rows, full=w_in, acc=w_acc, got=w_got, out=w_out, gather=True)
            )
        start += rows
    streams.append(
        dict(delay=COARSE_DELAY, first=0, rows=c_in.shape[0], full=c_in, acc=c_acc, got=c_got, out=c_out, gather=False)
    )
    for stream in streams:
        stream.update(at=stream["first"], landing=stream["first"], kept=[])

    def launch(which, stream, s):
        if s < count:
            mine, a, b = steps[s]
            size = stream["rows"] >> (s + 1)
            source = stream["full"] if s == 0 else stream["acc"]
            away = stream["at"] + (1 - mine) * size
            src = source.at[pl.ds(pl.multiple_of(away, 16), size)]
            dst = stream["got"].at[pl.ds(stream["landing"], size)]
        else:
            _, a, b = steps[2 * count - 1 - s]
            size = stream["rows"] >> (2 * count - s)
            src = stream["out"].at[pl.ds(pl.multiple_of(stream["kept"][2 * count - 1 - s], 16), size)]
            dst = src
        stream["copy"] = pltpu.make_async_remote_copy(
            src_ref=src, dst_ref=dst,
            send_sem=sems.at[0, which, s], recv_sem=sems.at[1, which, s],
            device_id=(a, b), device_id_type=MESH,
        )
        stream["copy"].start()

    def settle(stream, s):
        stream["copy"].wait()
        if s >= count:
            return
        mine = steps[s][0]
        size = stream["rows"] >> (s + 1)
        keep = stream["at"] + mine * size
        source = stream["full"] if s == 0 else stream["acc"]
        final = s == count - 1
        target = stream["out"] if final else stream["acc"]
        to = keep if stream["gather"] or not final else 0
        piece = stream["rows"] >> count
        add_into(target, to, source, keep, stream["got"], stream["landing"], size, piece)
        stream["at"] = keep
        stream["landing"] += size
        stream["kept"].append(keep)

    for slot in range(2 * count + max(CHUNKS, COARSE_DELAY) + 1):
        for which, stream in enumerate(streams):
            s = slot - stream["delay"]
            total = 2 * count if stream["gather"] else count
            if 1 <= s <= total:
                settle(stream, s - 1)
            if 0 <= s < total:
                launch(which, stream, s)
        if slot == 0:
            up.start()
            down.start()
            pl.when(has_before)(left.start)
            pl.when(has_after)(right.start)

            @pl.when(jnp.logical_not(has_after))
            def _():
                rec[2 * rows_y : 2 * rows_y + rows_x] = jnp.zeros((rows_x,) + rec.shape[1:], BF16)

            @pl.when(jnp.logical_not(has_before))
            def _():
                rec[2 * rows_y + rows_x :] = jnp.zeros((rows_x,) + rec.shape[1:], BF16)

    up.wait()
    down.wait()
    pl.when(has_before)(left.wait_send)
    pl.when(has_after)(left.wait_recv)
    pl.when(has_after)(right.wait_send)
    pl.when(has_before)(right.wait_recv)


def dot(left, right):
    return jnp.dot(left, right, preferred_element_type=F32)


def dot_t(left, right):
    return lax.dot_general(left, right, (((0,), (0,)), ((), ())), preferred_element_type=F32)


def dot_nt(left, right):
    return lax.dot_general(left, right, (((1,), (1,)), ((), ())), preferred_element_type=F32)


def silu_and_slope(value):
    sigma = jax.nn.sigmoid(value)
    return value * sigma, sigma * (1.0 + value * (1.0 - sigma))


def local_kernel(
    src_block, dst_block, own, rim, coarse, cot, w_src, w_dst, b_edge, w_msg, w_self, w_agg,
    b_node, w_out, src_idx, dst_idx, long_src, long_dst,
    base, g_own, g_rim, g_coarse, weights,
    table, sender, pre, act_sum, g_dst, g_table, half, d_src, d_bias,
):
    inner, block, width = own.shape
    rows = inner * block
    tiles = src_idx.shape[0]
    long_count = long_src.shape[1]
    span = GROUP * block
    table[:inner] = own[...]
    table[inner:] = rim[...]
    g_table[...] = jnp.zeros_like(g_table)
    g_dst[...] = jnp.zeros_like(g_dst)
    act_sum[...] = jnp.zeros_like(act_sum)
    d_src[...] = jnp.zeros_like(d_src)
    d_bias[...] = jnp.zeros_like(d_bias)
    own_rows = own[...].reshape(rows, width)
    half[...] = dot(own_rows, w_dst[...]).astype(BF16).reshape(inner, block, width)

    def hot(index, nodes):
        count = index.shape[1]
        return (lax.broadcasted_iota(jnp.int32, (nodes, count), 0) == index).astype(BF16)

    @pl.loop(0, tiles // GROUP)
    def _(g):
        first = pl.multiple_of(g * span, span)
        for j in range(GROUP):
            t = g * GROUP + j
            at = pl.ds(pl.multiple_of(first + j * block, block), block)
            sender[at, :] = dot_t(hot(src_idx[t], block), table[src_block[t]]).astype(BF16)
            pre[at, :] = dot_t(hot(dst_idx[t], block), half[dst_block[t]])
        at = pl.ds(first, span)
        value = dot(sender[at, :], w_src[...]) + pre[at, :] + b_edge[...]
        pre[at, :] = value
        act = (value * jax.nn.sigmoid(value)).astype(BF16)
        for j in range(GROUP):
            t = g * GROUP + j
            act_sum[dst_block[t]] += dot(
                hot(dst_idx[t], block), act[j * block : (j + 1) * block]
            )

    fine = tiles * block
    long_at = slice(fine, fine + long_count)
    long_hot = hot(long_dst[...], rows)
    sender[long_at, :] = dot_t(hot(long_src[...], coarse.shape[0]), coarse[...]).astype(BF16)
    value = (
        dot(sender[long_at, :], w_src[...])
        + dot_t(long_hot, half[...].reshape(rows, width))
        + b_edge[...]
    )
    pre[long_at, :] = value
    act = (value * jax.nn.sigmoid(value)).astype(BF16)
    acts = (act_sum[...].reshape(rows, width) + dot(long_hot, act)).astype(BF16)
    incoming = dot(acts, w_msg[...]).astype(BF16)
    node_pre = dot(own_rows, w_self[...]) + dot(incoming, w_agg[...]) + b_node[...]
    node_silu, node_slope = silu_and_slope(node_pre)
    cot_rows = cot[...].reshape(rows, width)
    cot_b = cot_rows.astype(BF16)

    def put(which, value):
        value = value.astype(BF16)
        for j in range(width // LANES):
            start = (which * (width // LANES) + j) * width
            weights[start : start + width, :] = value[:, j * LANES : (j + 1) * LANES]

    put(5, dot_t(node_silu.astype(BF16), cot_b))
    g_node = (dot_nt(cot_b, w_out[...]) * node_slope).astype(BF16)
    put(3, dot_t(own_rows, g_node))
    put(4, dot_t(incoming, g_node))
    d_node = jnp.sum(g_node.astype(F32), axis=0, keepdims=True)
    g_incoming = dot_nt(g_node, w_agg[...]).astype(BF16)
    put(2, dot_t(acts, g_incoming))
    base[...] = (cot_rows + dot_nt(g_node, w_self[...])).reshape(inner, block, width)
    half[...] = dot_nt(g_incoming, w_msg[...]).astype(BF16).reshape(inner, block, width)

    @pl.loop(0, tiles // GROUP)
    def _(g):
        first = pl.multiple_of(g * span, span)
        for j in range(GROUP):
            t = g * GROUP + j
            at = pl.ds(pl.multiple_of(first + j * block, block), block)
            dst_hot = hot(dst_idx[t], block)
            _, slope = silu_and_slope(pre[at, :])
            g_pre = (dot_t(dst_hot, half[dst_block[t]]) * slope).astype(BF16)
            pre[at, :] = g_pre.astype(F32)
            g_dst[dst_block[t]] += dot(dst_hot, g_pre)
            g_table[src_block[t]] += dot(hot(src_idx[t], block), g_pre)
        at = pl.ds(first, span)
        whole = pre[at, :]
        d_src[...] += dot_t(sender[at, :], whole.astype(BF16))
        d_bias[...] += jnp.sum(whole, axis=0, keepdims=True)

    _, slope = silu_and_slope(pre[long_at, :])
    long_hot = hot(long_dst[...], rows)
    g_pre = (dot_t(long_hot, half[...].reshape(rows, width)) * slope).astype(BF16)
    g_coarse[...] = dot(hot(long_src[...], coarse.shape[0]), g_pre).astype(BF16)
    put(0, d_src[...] + dot_t(sender[long_at, :], g_pre))
    d_edge = d_bias[...] + jnp.sum(g_pre.astype(F32), axis=0, keepdims=True)
    g_recv = (g_dst[...].reshape(rows, width) + dot(long_hot, g_pre)).astype(BF16)
    put(1, dot_t(own_rows, g_recv))
    base[...] += dot_nt(g_recv, w_dst[...]).reshape(inner, block, width)
    g_own[...] = g_table[:inner]
    g_rim[...] = g_table[inner:].astype(BF16)
    start = 6 * width * (width // LANES)
    tail = weights.shape[0] - start
    weights[start:, :] = jnp.zeros((tail, LANES), BF16)
    parts = [v[:, j * LANES : (j + 1) * LANES] for v in (d_edge, d_node) for j in range(width // LANES)]
    parts.append(jnp.zeros((16 - len(parts), LANES), F32))
    weights[start : start + 16, :] = jnp.concatenate(parts, axis=0).astype(BF16)


def finish_kernel(
    rows_x, rows_y, base, g_own, rec, c_sum, w_src, weights,
    grad, d_src, d_dst, b_edge, d_msg, d_self, d_agg, b_node, d_out, total,
):
    inner, block, width = base.shape
    rows = inner * block
    count = c_sum.shape[0]
    stride = rows // count
    node = lax.broadcasted_iota(jnp.int32, (rows, count), 0)
    place = lax.broadcasted_iota(jnp.int32, (rows, count), 1) * stride
    pick = (node == place).astype(BF16)
    total[...] = g_own[...] + dot(pick, c_sum[...]).reshape(inner, block, width)
    for c in range(rows_y):
        total[(rows_x - 1) * rows_y + c] += rec[c].astype(F32)
        total[c] += rec[rows_y + c].astype(F32)
    for r in range(rows_x):
        total[r * rows_y + rows_y - 1] += rec[2 * rows_y + r].astype(F32)
        total[r * rows_y] += rec[2 * rows_y + rows_x + r].astype(F32)
    sent = total[...].reshape(rows, width).astype(BF16)
    grad[...] = base[...] + dot_nt(sent, w_src[...]).reshape(inner, block, width)
    cols = width // LANES
    for which, ref in enumerate((d_src, d_dst, d_msg, d_self, d_agg, d_out)):
        for j in range(cols):
            start = (which * cols + j) * width
            ref[:, j * LANES : (j + 1) * LANES] = weights[start : start + width, :].astype(F32)
    start = 6 * width * cols
    bias = weights[start : start + 16, :].astype(F32)
    for j in range(cols):
        b_edge[:, j * LANES : (j + 1) * LANES] = bias[j : j + 1]
        b_node[:, j * LANES : (j + 1) * LANES] = bias[cols + j : cols + j + 1]


def vmem(count):
    return [pl.BlockSpec(memory_space=pltpu.VMEM)] * count


def body(
    n_px, n_py, latents, cotangent, w_src, w_dst, b_edge, w_msg, w_self, w_agg, b_node, w_out,
    src_block, dst_block, src_node, dst_node, long_src, long_dst,
):
    rows_x, rows_y, block, width = latents.shape
    inner = rows_x * rows_y
    nodes = inner * block
    rims = 2 * (rows_x + rows_y)
    tiles = src_block.shape[-1]
    long_count = long_src.shape[-1]
    edges = tiles * block + long_count
    devices = n_px * n_py
    stride = nodes // C_DEV
    steps = bits_of(n_px) + bits_of(n_py)
    coarse_count = C_DEV * devices
    exact = 6 * width * width // LANES + 16
    unit = 16 * devices
    w_rows = -(-exact // unit) * unit
    shape = jax.ShapeDtypeStruct
    dma = pltpu.SemaphoreType.DMA

    rounded = latents.astype(BF16)
    coarse_rows = latents.reshape(nodes, width)[::stride].astype(BF16)
    rim, coarse = pl.pallas_call(
        functools.partial(spread_kernel, n_px, n_py),
        out_shape=(shape((rims, block, width), BF16), shape((coarse_count, width), BF16)),
        in_specs=vmem(2),
        out_specs=tuple(vmem(2)),
        scratch_shapes=[dma((steps,)), dma((steps,)), dma((4,)), dma((4,))],
        compiler_params=pltpu.CompilerParams(collective_id=0, has_side_effects=True),
        name="spread",
    )(rounded, coarse_rows)

    owner = long_src.reshape(1, long_count) // C_DEV
    place = position_of(n_px, n_py, owner // n_py, owner % n_py)
    long_place = place * C_DEV + long_src.reshape(1, long_count) % C_DEV

    smem = [pl.BlockSpec(memory_space=pltpu.SMEM)] * 2
    base, g_own, g_rim, g_coarse, weights = pl.pallas_call(
        local_kernel,
        out_shape=(
            shape((inner, block, width), F32),
            shape((inner, block, width), F32),
            shape((rims, block, width), BF16),
            shape((coarse_count, width), BF16),
            shape((w_rows, LANES), BF16),
        ),
        in_specs=smem + vmem(16),
        out_specs=tuple(vmem(5)),
        scratch_shapes=[
            pltpu.VMEM((inner + rims, block, width), BF16),
            pltpu.VMEM((edges, width), BF16),
            pltpu.VMEM((edges, width), F32),
            pltpu.VMEM((inner, block, width), F32),
            pltpu.VMEM((inner, block, width), F32),
            pltpu.VMEM((inner + rims, block, width), F32),
            pltpu.VMEM((inner, block, width), BF16),
            pltpu.VMEM((width, width), F32),
            pltpu.VMEM((1, width), F32),
        ],
        compiler_params=pltpu.CompilerParams(vmem_limit_bytes=60 * 1024 * 1024),
        name="local",
    )(
        src_block.reshape(tiles), dst_block.reshape(tiles),
        rounded.reshape(inner, block, width), rim, coarse,
        cotangent.reshape(inner, block, width),
        w_src, w_dst, b_edge.reshape(1, width), w_msg, w_self, w_agg, b_node.reshape(1, width),
        w_out, src_node.reshape(tiles, 1, block), dst_node.reshape(tiles, 1, block),
        long_place, long_dst.reshape(1, long_count),
    )

    w_sum, c_sum, rec = pl.pallas_call(
        functools.partial(reduce_kernel, n_px, n_py, rows_x, rows_y),
        out_shape=(
            shape((w_rows, LANES), BF16),
            shape((C_DEV, width), BF16),
            shape((rims, block, width), BF16),
        ),
        in_specs=vmem(3),
        out_specs=tuple(vmem(3)),
        scratch_shapes=[
            pltpu.VMEM((w_rows, LANES), BF16),
            pltpu.VMEM((w_rows, LANES), BF16),
            pltpu.VMEM((coarse_count, width), BF16),
            pltpu.VMEM((coarse_count, width), BF16),
            dma((2, CHUNKS + 1, 2 * steps)), dma((2, 4)),
        ],
        compiler_params=pltpu.CompilerParams(
            collective_id=1, has_side_effects=True, vmem_limit_bytes=60 * 1024 * 1024
        ),
        name="reduce",
    )(weights, g_coarse, g_rim)

    matrix, vector = shape((width, width), F32), shape((1, width), F32)
    grad, d_src, d_dst, d_edge, d_msg, d_self, d_agg, d_node, d_out = pl.pallas_call(
        functools.partial(finish_kernel, rows_x, rows_y),
        out_shape=(
            shape((inner, block, width), F32),
            matrix, matrix, vector, matrix, matrix, matrix, vector, matrix,
        ),
        in_specs=vmem(6),
        out_specs=tuple(vmem(9)),
        scratch_shapes=[pltpu.VMEM((inner, block, width), F32)],
        compiler_params=pltpu.CompilerParams(vmem_limit_bytes=60 * 1024 * 1024),
        name="finish",
    )(base, g_own, rec, c_sum, w_src, w_sum)
    return (
        grad.reshape(latents.shape), d_src, d_dst, d_edge.reshape(width), d_msg, d_self, d_agg,
        d_node.reshape(width), d_out,
    )


def solution(mesh):
    n_px, n_py = mesh.shape["px"], mesh.shape["py"]
    part = {4: P("px", "py", None, None), 3: P("px", "py", None)}
    in_specs = (part[4], part[4]) + (P(),) * 8 + (part[3], part[3], part[4], part[4], part[3], part[3])
    out_specs = (part[4],) + (P(),) * 8
    return jax.shard_map(
        functools.partial(body, n_px, n_py),
        mesh=mesh, in_specs=in_specs, out_specs=out_specs, check_vma=False,
    )
```
